128 devices in a mesh: dev: 128 (over z, y, x, core).
Axes of the slice: x: 4, y: 4, z: 4, core: 2. Of those that a mesh axis runs over, the one named last changes fastest.
Arguments:
- source: bfloat16 [16384, 1024], P('dev'), may hold values from -17 to 17
- target: bfloat16 [16384, 1024], P('dev'), may hold values from -17 to 17
- partner: int32 [2, 128], replicated, may hold values from 0 to 127, as said below
Outputs:
- src_aligned: bfloat16 [16384, 1024], P('dev')
- tgt_aligned: bfloat16 [16384, 1024], P('dev')
- src_lse: float32 [16384], P('dev')
- tgt_lse: float32 [16384], P('dev')
The draws below stay inside these ranges and needn't reach their ends.
Inputs may be any that keep to these rules, and one draw needn't show every extreme that they name: Row r of partner is round r of one round-robin tournament among the 128 blocks: partner[r, partner[r, b]] = b and partner[r, b] != b; the rows are distinct rounds.
All inputs are finite; a program needn't handle non-finite values.
Results may differ from the reference program's by a relative error of at most 0.0018.
Values may be sent and summed in bfloat16 or wider, within the bound.
A program may use at most 64 MiB of HBM per device.

```python
import math
import jax
import jax.numpy as jnp
from jax import lax

D = 1024
ROWS = 128
ROUNDS = 2
BLOCKS = 128
TOTAL = 16384


def pairing(key):
    base = jax.random.fold_in(key, 101)
    perm_key, round_key = jax.random.split(base)
    slots = jax.random.permutation(perm_key, BLOCKS).astype(jnp.int32)
    chosen = jax.random.permutation(round_key, BLOCKS - 1)[:ROUNDS].astype(jnp.int32)
    owners = jnp.zeros((BLOCKS,), jnp.int32).at[slots].set(jnp.arange(BLOCKS, dtype=jnp.int32))
    final_slot = BLOCKS - 1

    def one_round(turn):
        other = jnp.mod(2 * turn - slots, final_slot)
        other = jnp.where(slots == turn, final_slot, other)
        other = jnp.where(slots == final_slot, turn, other)
        return owners[other]
    return jax.vmap(one_round)(chosen).astype(jnp.int32)


def embeddings(key):
    base = jax.random.fold_in(key, 202)
    streams = jax.random.split(base, 3)
    count = BLOCKS * ROWS

    def one_side(stream):
        pieces = jax.random.split(stream, 3)
        noise = jnp.clip(jax.random.normal(pieces[0], (count, D), jnp.float32), -3.0, 3.0)
        row_scale = jnp.exp(jax.random.uniform(pieces[1], (count, 1), jnp.float32, math.log(0.5), math.log(2.5)))
        col_scale = jnp.exp(jax.random.uniform(pieces[2], (1, D), jnp.float32, math.log(0.5), math.log(1.5)))
        return noise * col_scale * row_scale
    source = one_side(streams[1])
    target = one_side(streams[2])
    return (source, target)


def draw_source(key, part):
    return embeddings(key)[0].astype(jnp.bfloat16)


def draw_target(key, part):
    return embeddings(key)[1].astype(jnp.bfloat16)


def draw_partner(key, part):
    return pairing(key)


def setup_inputs(seed: int = 0) -> dict:
    seeds = jax.random.split(jax.random.key(seed), 4)
    source = draw_source(jax.random.fold_in(seeds[3], 71), 0)
    target = draw_target(jax.random.fold_in(seeds[3], 71), 0)
    partner = draw_partner(jax.random.fold_in(seeds[3], 71), 0)
    return dict(source=source, target=target, partner=partner)


def attend(queries, values, factor):
    scores = jnp.dot(queries, values.T, preferred_element_type=jnp.float32) * factor
    highest = jnp.max(scores, axis=1)
    weights = jnp.exp(scores - highest[:, None])
    summed_weights = jnp.sum(weights, axis=1)
    weighted = jnp.dot(weights.astype(jnp.bfloat16), values, preferred_element_type=jnp.float32)
    return highest, summed_weights, weighted


def merge_rounds(results):
    peak = results[0][0]
    for entry in results[1:]:
        peak = jnp.maximum(peak, entry[0])
    denominator = jnp.zeros_like(peak)
    numerator = jnp.zeros_like(results[0][2])
    for entry in results:
        factor = jnp.exp(entry[0] - peak)
        denominator = denominator + factor * entry[1]
        numerator = numerator + factor[:, None] * entry[2]
    return (numerator / denominator[:, None]).astype(jnp.bfloat16), peak + jnp.log(denominator)


def invert_row(order):
    return jnp.zeros((BLOCKS,), jnp.int32).at[order].set(jnp.arange(BLOCKS, dtype=jnp.int32))


def reference(source, target, partner):
    factor = D ** -0.5
    src_blocks = source.reshape(BLOCKS, ROWS, D)
    tgt_blocks = target.reshape(BLOCKS, ROWS, D)
    inverse = jax.vmap(invert_row)(partner)

    def source_block(block):
        results = [attend(src_blocks[block], tgt_blocks[partner[turn, block]], factor) for turn in range(ROUNDS)]
        return merge_rounds(results)

    def target_block(block):
        results = [attend(tgt_blocks[block], src_blocks[inverse[turn, block]], factor) for turn in range(ROUNDS)]
        return merge_rounds(results)

    numbers = jnp.arange(BLOCKS, dtype=jnp.int32)
    src_out, src_log = lax.map(source_block, numbers)
    tgt_out, tgt_log = lax.map(target_block, numbers)
    return (src_out.reshape(TOTAL, D), tgt_out.reshape(TOTAL, D),
            src_log.reshape(TOTAL), tgt_log.reshape(TOTAL))
```

```python
import functools

import jax
import jax.numpy as jnp
from jax import lax
from jax.experimental import pallas as pl
from jax.experimental.pallas import tpu as pltpu
from jax.sharding import PartitionSpec as P

MESH = pl.DeviceIdType.MESH
BF, F32 = jnp.bfloat16, jnp.float32


def tile(chip):
    row = pl.multiple_of(lax.div(chip, 8) * 16, 16)
    column = pl.multiple_of(lax.rem(chip, 8) * 128, 128)
    return pl.ds(row, 16), pl.ds(column, 128)


def attend(queries, values, factor):
    scores = lax.dot_general(
        queries, values, (((1,), (1,)), ((), ())), preferred_element_type=F32
    ) * factor
    highest = jnp.max(scores, axis=1, keepdims=True)
    weights = jnp.exp(scores - highest)
    total = jnp.sum(weights, axis=1, keepdims=True)
    summed = jnp.dot(weights.astype(BF), values, preferred_element_type=F32)
    return highest, total, summed


def to_row(column):
    rows = column.shape[0]
    at_row = lax.broadcasted_iota(jnp.int32, (rows, rows), 0)
    at_column = lax.broadcasted_iota(jnp.int32, (rows, rows), 1)
    spread = jnp.where(at_row == at_column, jnp.broadcast_to(column, (rows, rows)), 0.0)
    return jnp.sum(spread, axis=0, keepdims=True)


def side(query_ref, got, which, aligned_ref, lse_ref, factor):
    queries = query_ref[...]
    m0, t0, w0 = attend(queries, got[which, 0], factor)
    m1, t1, w1 = attend(queries, got[which, 1], factor)
    peak = jnp.maximum(m0, m1)
    f0, f1 = jnp.exp(m0 - peak), jnp.exp(m1 - peak)
    den = f0 * t0 + f1 * t1
    aligned_ref[...] = ((f0 * w0 + f1 * w1) / den).astype(BF)
    lse_ref[...] = to_row(peak + jnp.log(den))


def kernel(
    devices, factor, partner, s_ref, t_ref, so_ref, to_ref, sl_ref, tl_ref,
    held, stage, got, send1, recv1, send2, recv2, own_sem,
):
    chips = devices // 2
    me = lax.axis_index("dev")
    chip, core = lax.div(me, 2), lax.rem(me, 2)

    barrier = pltpu.get_barrier_semaphore()

    @pl.loop(1, devices)
    def _(k):
        pl.semaphore_signal(
            barrier, inc=1, device_id=(lax.rem(me + k, devices),), device_id_type=MESH
        )

    pl.semaphore_wait(barrier, devices - 1)

    def spread(ref, to_chip, to_core):
        rows, columns = tile(to_chip)
        return pltpu.make_async_remote_copy(
            src_ref=ref.at[rows, columns],
            dst_ref=held.at[me],
            send_sem=send1,
            recv_sem=recv1,
            device_id=(2 * to_chip + to_core,),
            device_id_type=MESH,
        )

    rows, columns = tile(chip)

    @pl.when(core == 0)
    def _():
        spread(t_ref, chip, 1).start()
        held[me] = s_ref[rows, columns]

    @pl.when(core == 1)
    def _():
        spread(s_ref, chip, 0).start()
        held[me] = t_ref[rows, columns]

    @pl.loop(1, chips)
    def _(k):
        to_chip = lax.rem(chip + k, chips)
        spread(s_ref, to_chip, 0).start()
        spread(t_ref, to_chip, 1).start()

    whole1 = held.at[pl.ds(0, devices - 1)]
    wait1 = pltpu.make_async_remote_copy(
        src_ref=whole1, dst_ref=whole1, send_sem=send1, recv_sem=recv1,
        device_id=(lax.rem(me + 1, devices),), device_id_type=MESH,
    )
    wait1.wait_recv()

    @pl.loop(1, devices)
    def _(k):
        j = lax.rem(me + k, devices)
        stage[j, 0] = held[partner[0, j]]
        stage[j, 1] = held[partner[1, j]]
        pltpu.make_async_remote_copy(
            src_ref=stage.at[j],
            dst_ref=got.at[core, :, rows, columns],
            send_sem=send2,
            recv_sem=recv2,
            device_id=(j,),
            device_id_type=MESH,
        ).start()

    got[core, 0, rows, columns] = held[partner[0, me]]
    got[core, 1, rows, columns] = held[partner[1, me]]
    whole2 = stage.at[pl.ds(0, devices - 1)]
    wait2 = pltpu.make_async_remote_copy(
        src_ref=whole2, dst_ref=whole2, send_sem=send2, recv_sem=recv2,
        device_id=(lax.rem(me + 1, devices),), device_id_type=MESH,
    )
    wait2.wait_recv()
    side(s_ref, got, 1, so_ref, sl_ref, factor)
    side(t_ref, got, 0, to_ref, tl_ref, factor)
    wait1.wait_send()
    wait2.wait_send()


def local(devices, source, target, partner):
    rows, width = source.shape
    vmem = pl.BlockSpec(memory_space=pltpu.VMEM)
    so, to, sl, tl = pl.pallas_call(
        functools.partial(kernel, devices, width ** (-0.5)),
        out_shape=(
            jax.ShapeDtypeStruct((rows, width), BF),
            jax.ShapeDtypeStruct((rows, width), BF),
            jax.ShapeDtypeStruct((1, rows), F32),
            jax.ShapeDtypeStruct((1, rows), F32),
        ),
        in_specs=[pl.BlockSpec(memory_space=pltpu.SMEM), vmem, vmem],
        out_specs=(vmem, vmem, vmem, vmem),
        scratch_shapes=[
            pltpu.VMEM((devices, 16, 128), BF),
            pltpu.VMEM((devices, 2, 16, 128), BF),
            pltpu.VMEM((2, 2, rows, width), BF),
            pltpu.SemaphoreType.DMA,
            pltpu.SemaphoreType.DMA,
            pltpu.SemaphoreType.DMA,
            pltpu.SemaphoreType.DMA,
            pltpu.SemaphoreType.DMA,
        ],
        compiler_params=pltpu.CompilerParams(collective_id=0, has_side_effects=True),
    )(partner, source, target)
    return so, to, sl.reshape(rows), tl.reshape(rows)


def solution(mesh):
    devices = mesh.shape["dev"]
    return jax.shard_map(
        functools.partial(local, devices),
        mesh=mesh,
        in_specs=(P("dev", None), P("dev", None), P()),
        out_specs=(P("dev", None), P("dev", None), P("dev"), P("dev")),
        check_vma=False,
    )
```

```python
import functools

import jax
import jax.numpy as jnp
from jax import lax
from jax.experimental import pallas as pl
from jax.experimental.pallas import tpu as pltpu
from jax.sharding import PartitionSpec as P

MESH = pl.DeviceIdType.MESH
BF, F32 = jnp.bfloat16, jnp.float32
SIDE = 4
CHIPS = SIDE * SIDE * SIDE
DEVICES = 2 * CHIPS
WIDE = 256


def tile(chip):
    row = pl.multiple_of(lax.div(chip, 8) * 16, 16)
    column = pl.multiple_of(lax.rem(chip, 8) * 128, 128)
    return pl.ds(row, 16), pl.ds(column, 128)


def shifted(chip, offset):
    z = lax.rem(lax.div(chip, 16) + lax.div(offset, 16), 4)
    y = lax.rem(lax.div(chip, 4) + lax.div(offset, 4), 4)
    x = lax.rem(chip + offset, 4)
    return 16 * z + 4 * y + x


def weigh(queries, values, factor):
    scores = lax.dot_general(
        queries, values, (((1,), (1,)), ((), ())), preferred_element_type=F32
    ) * factor
    highest = jnp.max(scores, axis=1, keepdims=True)
    weights = jnp.exp(scores - highest)
    total = jnp.sum(weights, axis=1, keepdims=True)
    return highest, total, weights.astype(BF)


def to_row(column):
    rows = column.shape[0]
    at_row = lax.broadcasted_iota(jnp.int32, (rows, rows), 0)
    at_column = lax.broadcasted_iota(jnp.int32, (rows, rows), 1)
    spread = jnp.where(at_row == at_column, jnp.broadcast_to(column, (rows, rows)), 0.0)
    return jnp.sum(spread, axis=0, keepdims=True)


def kernel(
    factor, partner, s_hbm, t_hbm, so_hbm, to_hbm, lse_ref,
    s_ref, t_ref, so_ref, to_ref, first, held, stage, got,
    send1, recv1, send2, recv2, in_sem, out_sem,
):
    me = lax.axis_index("dev")
    chip, core = lax.div(me, 2), lax.rem(me, 2)
    rows, columns = tile(chip)

    get_s = pltpu.make_async_copy(s_hbm, s_ref, in_sem.at[0])
    get_t = pltpu.make_async_copy(t_hbm, t_ref, in_sem.at[1])
    get_s.start()
    get_t.start()

    barrier = pltpu.get_barrier_semaphore()

    @pl.loop(1, DEVICES)
    def _(k):
        pl.semaphore_signal(
            barrier, inc=1, device_id=(lax.rem(me + k, DEVICES),), device_id_type=MESH
        )

    get_s.wait()
    get_t.wait()
    pl.semaphore_wait(barrier, DEVICES - 1)

    def spread(ref, to_chip, to_core):
        at_rows, at_columns = tile(to_chip)
        pltpu.make_async_remote_copy(
            src_ref=ref.at[at_rows, at_columns],
            dst_ref=held.at[me],
            send_sem=send1,
            recv_sem=recv1,
            device_id=(2 * to_chip + to_core,),
            device_id_type=MESH,
        ).start()

    def keep(ref):
        pltpu.make_async_copy(ref.at[rows, columns], held.at[me], recv1).start()

    for to_core, ref in ((0, s_ref), (1, t_ref)):
        @pl.when(core == to_core)
        def _():
            keep(ref)

        @pl.when(core != to_core)
        def _():
            spread(ref, chip, to_core)

        @pl.loop(1, CHIPS)
        def _(k):
            spread(ref, shifted(chip, lax.rem(k * 27, CHIPS)), to_core)

    pltpu.make_async_copy(held, held, recv1).wait()

    def fetch(turn, j):
        stage[j, turn] = held[partner[turn, j]]

    def both(j):
        return stage.at[j], got.at[0, :, rows, columns], recv2.at[0]

    def one(turn, j):
        return stage.at[j, turn], got.at[1, turn, rows, columns], recv2.at[1 + turn]

    def collect(turns, parts):
        for turn in turns:
            fetch(turn, me)
        src, dst, sem = parts(me)
        pltpu.make_async_copy(src, dst, sem).start()

        @pl.loop(1, DEVICES)
        def _(k):
            offset = lax.rem(k * 53, DEVICES)
            j = 2 * shifted(chip, lax.div(offset, 2)) + lax.rem(core + offset, 2)
            for turn in turns:
                fetch(turn, j)
            src, dst, sem = parts(j)
            pltpu.make_async_remote_copy(
                src_ref=src, dst_ref=dst, send_sem=send2, recv_sem=sem,
                device_id=(j,), device_id_type=MESH,
            ).start()

    @pl.when(core == 0)
    def _():
        collect((0, 1), both)

    @pl.when(core == 1)
    def _():
        collect((0,), functools.partial(one, 0))
        collect((1,), functools.partial(one, 1))

    def part(which, turn, weights, at):
        return jnp.dot(weights, got[which, turn, :, at], preferred_element_type=F32)

    def merged(m0, t0, m1, t1):
        peak = jnp.maximum(m0, m1)
        f0, f1 = jnp.exp(m0 - peak), jnp.exp(m1 - peak)
        den = f0 * t0 + f1 * t1
        return f0, f1, 1.0 / den, to_row(peak + jnp.log(den))

    chunks = [slice(at, at + WIDE) for at in range(0, s_ref.shape[1], WIDE)]

    pltpu.make_async_copy(got.at[0], got.at[0], recv2.at[0]).wait()
    queries = t_ref[...]
    m0, t0, p0 = weigh(queries, got[0, 0], factor)
    m1, t1, p1 = weigh(queries, got[0, 1], factor)
    f0, f1, inverse, lse = merged(m0, t0, m1, t1)
    for at in chunks:
        to_ref[:, at] = ((f0 * part(0, 0, p0, at) + f1 * part(0, 1, p1, at)) * inverse).astype(BF)
    put_t = pltpu.make_async_copy(to_ref, to_hbm, out_sem.at[1])
    put_t.start()
    lse_ref[1:2] = lse

    pltpu.make_async_copy(got.at[1, 0], got.at[1, 0], recv2.at[1]).wait()
    queries = s_ref[...]
    m0, t0, p0 = weigh(queries, got[1, 0], factor)
    for at in chunks:
        first[:, at] = part(1, 0, p0, at)

    pltpu.make_async_copy(got.at[1, 1], got.at[1, 1], recv2.at[2]).wait()
    m1, t1, p1 = weigh(queries, got[1, 1], factor)
    f0, f1, inverse, lse = merged(m0, t0, m1, t1)
    for at in chunks:
        so_ref[:, at] = ((f0 * first[:, at] + f1 * part(1, 1, p1, at)) * inverse).astype(BF)
    put_s = pltpu.make_async_copy(so_ref, so_hbm, out_sem.at[0])
    put_s.start()
    lse_ref[0:1] = lse

    def sent(ref, sem):
        pltpu.make_async_remote_copy(
            src_ref=ref, dst_ref=ref, send_sem=sem, recv_sem=sem,
            device_id=(lax.rem(me + 1, DEVICES),), device_id_type=MESH,
        ).wait_send()

    sent(held.at[pl.ds(0, DEVICES - 1)], send1)
    sent(stage.at[pl.ds(0, DEVICES - 1)], send2)
    put_t.wait()
    put_s.wait()


def hand_on(s_ref, t_ref, lse_ref, so_ref, to_ref, sl_ref, tl_ref, s_buf, t_buf, sems):
    ins = [
        pltpu.make_async_copy(s_ref, s_buf, sems.at[0]),
        pltpu.make_async_copy(t_ref, t_buf, sems.at[1]),
    ]
    outs = [
        pltpu.make_async_copy(s_buf, so_ref, sems.at[2]),
        pltpu.make_async_copy(t_buf, to_ref, sems.at[3]),
    ]
    for copy in ins:
        copy.start()
    sl_ref[...] = lse_ref[0]
    tl_ref[...] = lse_ref[1]
    for there, back in zip(ins, outs):
        there.wait()
        back.start()
    for copy in outs:
        copy.wait()


def local(source, target, partner):
    rows, width = source.shape
    vmem = pl.BlockSpec(memory_space=pltpu.VMEM)
    anywhere = pl.BlockSpec(memory_space=pl.ANY)
    slab = jax.ShapeDtypeStruct((rows, width), BF)
    row = jax.ShapeDtypeStruct((rows,), F32)
    aligned_s, aligned_t, lse = pl.pallas_call(
        functools.partial(kernel, width ** (-0.5)),
        out_shape=(slab, slab, jax.ShapeDtypeStruct((2, rows), F32)),
        in_specs=[pl.BlockSpec(memory_space=pltpu.SMEM), anywhere, anywhere],
        out_specs=(anywhere, anywhere, vmem),
        scratch_shapes=[
            pltpu.VMEM((rows, width), BF),
            pltpu.VMEM((rows, width), BF),
            pltpu.VMEM((rows, width), BF),
            pltpu.VMEM((rows, width), BF),
            pltpu.VMEM((rows, width), F32),
            pltpu.VMEM((DEVICES, 16, 128), BF),
            pltpu.VMEM((DEVICES, 2, 16, 128), BF),
            pltpu.VMEM((2, 2, rows, width), BF),
            pltpu.SemaphoreType.DMA,
            pltpu.SemaphoreType.DMA,
            pltpu.SemaphoreType.DMA,
            pltpu.SemaphoreType.DMA((3,)),
            pltpu.SemaphoreType.DMA((2,)),
            pltpu.SemaphoreType.DMA((2,)),
        ],
        compiler_params=pltpu.CompilerParams(collective_id=0, has_side_effects=True),
    )(partner, source, target)
    return pl.pallas_call(
        hand_on,
        out_shape=(slab, slab, row, row),
        in_specs=[anywhere, anywhere, vmem],
        out_specs=(anywhere, anywhere, vmem, vmem),
        scratch_shapes=[
            pltpu.VMEM((rows, width), BF),
            pltpu.VMEM((rows, width), BF),
            pltpu.SemaphoreType.DMA((4,)),
        ],
    )(aligned_s, aligned_t, lse)


def solution(mesh):
    return jax.shard_map(
        local,
        mesh=mesh,
        in_specs=(P("dev", None), P("dev", None), P()),
        out_specs=(P("dev", None), P("dev", None), P("dev"), P("dev")),
        check_vma=False,
    )
```

```python
import functools

import jax
import jax.numpy as jnp
from jax import lax
from jax.experimental import pallas as pl
from jax.experimental.pallas import tpu as pltpu
from jax.sharding import PartitionSpec as P

MESH = pl.DeviceIdType.MESH
BF, F32 = jnp.bfloat16, jnp.float32
SIDE = 4
DEVICES = 2 * SIDE**3
WIDE = 256
HOPS = (0, 1, 2, 1)
FAR_FIRST = sorted(
    ((z, y, x) for z in range(SIDE) for y in range(SIDE) for x in range(SIDE)),
    key=lambda offset: -sum(HOPS[step] for step in offset),
)[:-1]


def tile(chip):
    row = pl.multiple_of(lax.div(chip, 8) * 16, 16)
    column = pl.multiple_of(lax.rem(chip, 8) * 128, 128)
    return pl.ds(row, 16), pl.ds(column, 128)


def away(place, offset):
    z, y, x = (lax.rem(at + step, SIDE) if step else at for at, step in zip(place, offset))
    return (SIDE * z + y) * SIDE + x


def weigh(queries, values, factor):
    scores = lax.dot_general(
        queries, values, (((1,), (1,)), ((), ())), preferred_element_type=F32
    ) * factor
    highest = jnp.max(scores, axis=1, keepdims=True)
    weights = jnp.exp(scores - highest)
    total = jnp.sum(weights, axis=1, keepdims=True)
    return highest, total, weights.astype(BF)


def to_row(column):
    rows = column.shape[0]
    at_row = lax.broadcasted_iota(jnp.int32, (rows, rows), 0)
    at_column = lax.broadcasted_iota(jnp.int32, (rows, rows), 1)
    spread = jnp.where(at_row == at_column, jnp.broadcast_to(column, (rows, rows)), 0.0)
    return jnp.sum(spread, axis=0, keepdims=True)


def kernel(
    factor, partner, s_hbm, t_hbm, so_hbm, to_hbm, lse_ref,
    s_ref, t_ref, so_ref, to_ref, held, stage, got,
    send1, recv1, send2, recv2, in_sem, out_sem,
):
    me = lax.axis_index("dev")
    chip, core = lax.div(me, 2), lax.rem(me, 2)
    place = tuple(lax.rem(lax.div(chip, unit), SIDE) for unit in (SIDE * SIDE, SIDE, 1))
    mate = 2 * chip + 1 - core
    rows, columns = tile(chip)

    get_s = pltpu.make_async_copy(s_hbm, s_ref, in_sem.at[0])
    get_t = pltpu.make_async_copy(t_hbm, t_ref, in_sem.at[1])
    get_s.start()
    get_t.start()

    barrier = pltpu.get_barrier_semaphore()

    def others():
        for offset in FAR_FIRST:
            first_core = 2 * away(place, offset)
            yield first_core
            yield first_core + 1
        yield mate

    for j in others():
        pl.semaphore_signal(barrier, inc=1, device_id=(j,), device_id_type=MESH)

    get_s.wait()
    get_t.wait()
    pl.semaphore_wait(barrier, DEVICES - 1)

    def spread(ref, to_chip, to_core):
        at_rows, at_columns = tile(to_chip)
        pltpu.make_async_remote_copy(
            src_ref=ref.at[at_rows, at_columns],
            dst_ref=held.at[me],
            send_sem=send1,
            recv_sem=recv1,
            device_id=(2 * to_chip + to_core,),
            device_id_type=MESH,
        ).start()

    def keep(ref):
        pltpu.make_async_copy(ref.at[rows, columns], held.at[me], recv1).start()

    for to_core, ref in ((0, s_ref), (1, t_ref)):
        @pl.when(core == to_core)
        def _():
            keep(ref)

        @pl.when(core != to_core)
        def _():
            spread(ref, chip, to_core)

        for offset in FAR_FIRST:
            spread(ref, away(place, offset), to_core)

    pltpu.make_async_copy(held, held, recv1).wait()

    def fetch(j):
        for turn in range(2):
            stage[j, turn] = held[partner[turn, j]]

    fetch(me)
    pltpu.make_async_copy(
        stage.at[me], got.at[core, :, rows, columns], recv2.at[core]
    ).start()
    for j in others():
        fetch(j)
        pltpu.make_async_remote_copy(
            src_ref=stage.at[j],
            dst_ref=got.at[core, :, rows, columns],
            send_sem=send2,
            recv_sem=recv2.at[core],
            device_id=(j,),
            device_id_type=MESH,
        ).start()

    def part(which, turn, weights, at):
        return jnp.dot(weights, got[which, turn, :, at], preferred_element_type=F32)

    def merged(m0, t0, m1, t1):
        peak = jnp.maximum(m0, m1)
        f0, f1 = jnp.exp(m0 - peak), jnp.exp(m1 - peak)
        den = f0 * t0 + f1 * t1
        return f0, f1, 1.0 / den, to_row(peak + jnp.log(den))

    chunks = [slice(at, at + WIDE) for at in range(0, s_ref.shape[1], WIDE)]

    def side(which, query_ref, aligned_ref, slab, row):
        pltpu.make_async_copy(got.at[which], got.at[which], recv2.at[which]).wait()
        queries = query_ref[...]
        m0, t0, p0 = weigh(queries, got[which, 0], factor)
        m1, t1, p1 = weigh(queries, got[which, 1], factor)
        f0, f1, inverse, lse = merged(m0, t0, m1, t1)
        for at in chunks:
            total = f0 * part(which, 0, p0, at) + f1 * part(which, 1, p1, at)
            aligned_ref[:, at] = (total * inverse).astype(BF)
        lse_ref[row : row + 1] = lse
        put = pltpu.make_async_copy(aligned_ref, slab, out_sem.at[row])
        put.start()
        return put

    put_t = side(0, t_ref, to_ref, to_hbm, 1)
    put_s = side(1, s_ref, so_ref, so_hbm, 0)

    def sent(ref, sem):
        pltpu.make_async_remote_copy(
            src_ref=ref, dst_ref=ref, send_sem=sem, recv_sem=sem,
            device_id=(lax.rem(me + 1, DEVICES),), device_id_type=MESH,
        ).wait_send()

    sent(held.at[pl.ds(0, DEVICES - 1)], send1)
    sent(stage.at[pl.ds(0, DEVICES - 1)], send2)
    put_t.wait()
    put_s.wait()


def hand_on(s_ref, t_ref, lse_ref, so_ref, to_ref, sl_ref, tl_ref):
    so_ref[...] = s_ref[...]
    to_ref[...] = t_ref[...]
    sl_ref[...] = lse_ref[0]
    tl_ref[...] = lse_ref[1]


def local(source, target, partner):
    rows, width = source.shape
    vmem = pl.BlockSpec(memory_space=pltpu.VMEM)
    anywhere = pl.BlockSpec(memory_space=pl.ANY)
    slab = jax.ShapeDtypeStruct((rows, width), BF)
    row = jax.ShapeDtypeStruct((rows,), F32)
    aligned_s, aligned_t, lse = pl.pallas_call(
        functools.partial(kernel, width ** (-0.5)),
        out_shape=(slab, slab, jax.ShapeDtypeStruct((2, rows), F32)),
        in_specs=[pl.BlockSpec(memory_space=pltpu.SMEM), anywhere, anywhere],
        out_specs=(anywhere, anywhere, vmem),
        scratch_shapes=[
            pltpu.VMEM((rows, width), BF),
            pltpu.VMEM((rows, width), BF),
            pltpu.VMEM((rows, width), BF),
            pltpu.VMEM((rows, width), BF),
            pltpu.VMEM((DEVICES, 16, 128), BF),
            pltpu.VMEM((DEVICES, 2, 16, 128), BF),
            pltpu.VMEM((2, 2, rows, width), BF),
            pltpu.SemaphoreType.DMA,
            pltpu.SemaphoreType.DMA,
            pltpu.SemaphoreType.DMA,
            pltpu.SemaphoreType.DMA((2,)),
            pltpu.SemaphoreType.DMA((2,)),
            pltpu.SemaphoreType.DMA((2,)),
        ],
        compiler_params=pltpu.CompilerParams(collective_id=0, has_side_effects=True),
    )(partner, source, target)
    return pl.pallas_call(
        hand_on,
        out_shape=(slab, slab, row, row),
        in_specs=[vmem, vmem, vmem],
        out_specs=(vmem, vmem, vmem, vmem),
    )(aligned_s, aligned_t, lse)


def solution(mesh):
    return jax.shard_map(
        local,
        mesh=mesh,
        in_specs=(P("dev", None), P("dev", None), P()),
        out_specs=(P("dev", None), P("dev", None), P("dev"), P("dev")),
        check_vma=False,
    )
```

```python
import functools

import jax
import jax.numpy as jnp
from jax import lax
from jax.experimental import pallas as pl
from jax.experimental.pallas import tpu as pltpu
from jax.sharding import PartitionSpec as P

MESH = pl.DeviceIdType.MESH
BF, F32 = jnp.bfloat16, jnp.float32
SIDE = 4
DEVICES = 2 * SIDE**3
WIDE = 256
GRANT = 54700 << 10
HOPS = (0, 1, 2, 1)
FAR_FIRST = sorted(
    ((z, y, x) for z in range(SIDE) for y in range(SIDE) for x in range(SIDE)),
    key=lambda offset: -sum(HOPS[step] for step in offset),
)[:-1]


def tile(chip):
    row = pl.multiple_of(lax.div(chip, 8) * 16, 16)
    column = pl.multiple_of(lax.rem(chip, 8) * 128, 128)
    return pl.ds(row, 16), pl.ds(column, 128)


def away(place, offset):
    z, y, x = (lax.rem(at + step, SIDE) if step else at for at, step in zip(place, offset))
    return (SIDE * z + y) * SIDE + x


def weigh(queries, values, factor):
    scores = lax.dot_general(
        queries, values, (((1,), (1,)), ((), ())), preferred_element_type=F32
    ) * factor
    highest = jnp.max(scores, axis=1, keepdims=True)
    weights = jnp.exp(scores - highest)
    total = jnp.sum(weights, axis=1, keepdims=True)
    return highest, total, weights.astype(BF)


def to_row(column):
    rows = column.shape[0]
    at_row = lax.broadcasted_iota(jnp.int32, (rows, rows), 0)
    at_column = lax.broadcasted_iota(jnp.int32, (rows, rows), 1)
    spread = jnp.where(at_row == at_column, jnp.broadcast_to(column, (rows, rows)), 0.0)
    return jnp.sum(spread, axis=0, keepdims=True)


def kernel(
    factor, partner_hbm, s_hbm, t_hbm, so_ref, to_ref, lse_ref,
    partner, s_ref, t_ref, held, stage, got,
    send1, recv1, send2, recv2, in_sem,
):
    me = lax.axis_index("dev")
    chip, core = lax.div(me, 2), lax.rem(me, 2)
    place = tuple(lax.rem(lax.div(chip, unit), SIDE) for unit in (SIDE * SIDE, SIDE, 1))
    mate = 2 * chip + 1 - core
    rows, columns = tile(chip)

    get_s = pltpu.make_async_copy(s_hbm, s_ref, in_sem.at[0])
    get_t = pltpu.make_async_copy(t_hbm, t_ref, in_sem.at[1])
    get_partner = pltpu.make_async_copy(partner_hbm, partner, in_sem.at[2])
    get_s.start()
    get_t.start()
    get_partner.start()

    barrier = pltpu.get_barrier_semaphore()

    def others():
        for offset in FAR_FIRST:
            first_core = 2 * away(place, offset)
            yield first_core
            yield first_core + 1
        yield mate

    for j in others():
        pl.semaphore_signal(barrier, inc=1, device_id=(j,), device_id_type=MESH)

    get_partner.wait()
    get_s.wait()
    get_t.wait()
    pl.semaphore_wait(barrier, DEVICES - 1)

    def spread(ref, to_chip, to_core):
        at_rows, at_columns = tile(to_chip)
        pltpu.make_async_remote_copy(
            src_ref=ref.at[at_rows, at_columns],
            dst_ref=held.at[me],
            send_sem=send1,
            recv_sem=recv1,
            device_id=(2 * to_chip + to_core,),
            device_id_type=MESH,
        ).start()

    def keep(ref):
        pltpu.make_async_copy(ref.at[rows, columns], held.at[me], recv1).start()

    for to_core, ref in ((0, s_ref), (1, t_ref)):
        @pl.when(core == to_core)
        def _():
            keep(ref)

        @pl.when(core != to_core)
        def _():
            spread(ref, chip, to_core)

        for offset in FAR_FIRST:
            spread(ref, away(place, offset), to_core)

    pltpu.make_async_copy(held, held, recv1).wait()

    def fetch(j):
        for turn in range(2):
            stage[j, turn] = held[partner[turn, j]]

    fetch(me)
    pltpu.make_async_copy(
        stage.at[me], got.at[core, :, rows, columns], recv2.at[core]
    ).start()
    for j in others():
        fetch(j)
        pltpu.make_async_remote_copy(
            src_ref=stage.at[j],
            dst_ref=got.at[core, :, rows, columns],
            send_sem=send2,
            recv_sem=recv2.at[core],
            device_id=(j,),
            device_id_type=MESH,
        ).start()

    def part(which, turn, weights, at):
        return jnp.dot(weights, got[which, turn, :, at], preferred_element_type=F32)

    def merged(m0, t0, m1, t1):
        peak = jnp.maximum(m0, m1)
        f0, f1 = jnp.exp(m0 - peak), jnp.exp(m1 - peak)
        den = f0 * t0 + f1 * t1
        return f0, f1, 1.0 / den, to_row(peak + jnp.log(den))

    chunks = [slice(at, at + WIDE) for at in range(0, s_ref.shape[1], WIDE)]

    def side(which, query_ref, aligned_ref, row):
        pltpu.make_async_copy(got.at[which], got.at[which], recv2.at[which]).wait()
        queries = query_ref[...]
        m0, t0, p0 = weigh(queries, got[which, 0], factor)
        m1, t1, p1 = weigh(queries, got[which, 1], factor)
        f0, f1, inverse, lse = merged(m0, t0, m1, t1)
        for at in chunks:
            total = f0 * part(which, 0, p0, at) + f1 * part(which, 1, p1, at)
            aligned_ref[:, at] = (total * inverse).astype(BF)
        lse_ref[row : row + 1] = lse

    side(0, t_ref, to_ref, 1)
    side(1, s_ref, so_ref, 0)

    def sent(ref, sem):
        pltpu.make_async_remote_copy(
            src_ref=ref, dst_ref=ref, send_sem=sem, recv_sem=sem,
            device_id=(lax.rem(me + 1, DEVICES),), device_id_type=MESH,
        ).wait_send()

    sent(held.at[pl.ds(0, DEVICES - 1)], send1)
    sent(stage.at[pl.ds(0, DEVICES - 1)], send2)


def hand_on(s_ref, t_ref, lse_ref, so_ref, to_ref, sl_ref, tl_ref):
    so_ref[...] = s_ref[...]
    to_ref[...] = t_ref[...]
    sl_ref[...] = lse_ref[0]
    tl_ref[...] = lse_ref[1]


def local(source, target, partner):
    rows, width = source.shape
    vmem = pl.BlockSpec(memory_space=pltpu.VMEM)
    anywhere = pl.BlockSpec(memory_space=pl.ANY)
    slab = jax.ShapeDtypeStruct((rows, width), BF)
    row = jax.ShapeDtypeStruct((rows,), F32)
    aligned_s, aligned_t, lse = pl.pallas_call(
        functools.partial(kernel, width ** (-0.5)),
        out_shape=(slab, slab, jax.ShapeDtypeStruct((2, rows), F32)),
        in_specs=[anywhere, anywhere, anywhere],
        out_specs=(vmem, vmem, vmem),
        scratch_shapes=[
            pltpu.SMEM(partner.shape, jnp.int32),
            pltpu.VMEM((rows, width), BF),
            pltpu.VMEM((rows, width), BF),
            pltpu.VMEM((DEVICES, 16, 128), BF),
            pltpu.VMEM((DEVICES, 2, 16, 128), BF),
            pltpu.VMEM((2, 2, rows, width), BF),
            pltpu.SemaphoreType.DMA,
            pltpu.SemaphoreType.DMA,
            pltpu.SemaphoreType.DMA,
            pltpu.SemaphoreType.DMA((2,)),
            pltpu.SemaphoreType.DMA((3,)),
        ],
        compiler_params=pltpu.CompilerParams(
            collective_id=0, has_side_effects=True, vmem_limit_bytes=GRANT
        ),
    )(partner, source, target)
    return pl.pallas_call(
        hand_on,
        out_shape=(slab, slab, row, row),
        in_specs=[vmem, vmem, vmem],
        out_specs=(vmem, vmem, vmem, vmem),
        compiler_params=pltpu.CompilerParams(vmem_limit_bytes=GRANT),
    )(aligned_s, aligned_t, lse)


def solution(mesh):
    return jax.shard_map(
        local,
        mesh=mesh,
        in_specs=(P("dev", None), P("dev", None), P()),
        out_specs=(P("dev", None), P("dev", None), P("dev"), P("dev")),
        check_vma=False,
    )
```

```python
import functools

import jax
import jax.numpy as jnp
from jax import lax
from jax.experimental import pallas as pl
from jax.experimental.pallas import tpu as pltpu
from jax.sharding import PartitionSpec as P

MESH = pl.DeviceIdType.MESH
BF, F32 = jnp.bfloat16, jnp.float32
SIDE = 4
DEVICES = 2 * SIDE**3
WIDE = 256
GRANT = 54700 << 10
HOPS = (0, 1, 2, 1)
FAR_FIRST = sorted(
    ((z, y, x) for z in range(SIDE) for y in range(SIDE) for x in range(SIDE)),
    key=lambda offset: -sum(HOPS[step] for step in offset),
)[:-1]


def tile(device):
    row = pl.multiple_of(lax.div(device, 8) * 8, 8)
    column = pl.multiple_of(lax.rem(device, 8) * 128, 128)
    return pl.ds(row, 8), pl.ds(column, 128)


def away(place, offset):
    z, y, x = (lax.rem(at + step, SIDE) if step else at for at, step in zip(place, offset))
    return (SIDE * z + y) * SIDE + x


def weigh(queries, values, factor):
    scores = lax.dot_general(
        queries, values, (((1,), (1,)), ((), ())), preferred_element_type=F32
    ) * factor
    highest = jnp.max(scores, axis=1, keepdims=True)
    weights = jnp.exp(scores - highest)
    total = jnp.sum(weights, axis=1, keepdims=True)
    return highest, total, weights.astype(BF)


def to_row(column):
    rows = column.shape[0]
    at_row = lax.broadcasted_iota(jnp.int32, (rows, rows), 0)
    at_column = lax.broadcasted_iota(jnp.int32, (rows, rows), 1)
    spread = jnp.where(at_row == at_column, jnp.broadcast_to(column, (rows, rows)), 0.0)
    return jnp.sum(spread, axis=0, keepdims=True)


def kernel(
    factor, partner_hbm, s_hbm, t_hbm, so_ref, to_ref, lse_ref,
    partner, s_ref, t_ref, held_s, held_t, stage, got,
    send1, recv1, send2, recv2, in_sem,
):
    me = lax.axis_index("dev")
    chip, core = lax.div(me, 2), lax.rem(me, 2)
    place = tuple(lax.rem(lax.div(chip, unit), SIDE) for unit in (SIDE * SIDE, SIDE, 1))
    mate = 2 * chip + 1 - core
    rows, columns = tile(me)

    get_s = pltpu.make_async_copy(s_hbm, s_ref, in_sem.at[0])
    get_t = pltpu.make_async_copy(t_hbm, t_ref, in_sem.at[1])
    get_partner = pltpu.make_async_copy(partner_hbm, partner, in_sem.at[2])
    get_s.start()
    get_t.start()
    get_partner.start()

    barrier = pltpu.get_barrier_semaphore()

    def others():
        for offset in FAR_FIRST:
            first_core = 2 * away(place, offset)
            yield first_core
            yield first_core + 1
        yield mate

    for j in others():
        pl.semaphore_signal(barrier, inc=1, device_id=(j,), device_id_type=MESH)

    get_partner.wait()
    get_s.wait()
    get_t.wait()
    pl.semaphore_wait(barrier, DEVICES - 1)

    sides = ((0, s_ref, held_s), (1, t_ref, held_t))

    for which, ref, held in sides:
        pltpu.make_async_copy(
            ref.at[rows, columns], held.at[me], recv1.at[which]
        ).start()
        for j in others():
            at_rows, at_columns = tile(j)
            pltpu.make_async_remote_copy(
                src_ref=ref.at[at_rows, at_columns],
                dst_ref=held.at[me],
                send_sem=send1.at[which],
                recv_sem=recv1.at[which],
                device_id=(j,),
                device_id_type=MESH,
            ).start()

    for which, ref, held in sides:
        pltpu.make_async_copy(held, held, recv1.at[which]).wait()

        def fetch(j):
            for turn in range(2):
                stage[which, j, turn] = held[partner[turn, j]]

        fetch(me)
        pltpu.make_async_copy(
            stage.at[which, me], got.at[which, :, rows, columns], recv2.at[which]
        ).start()
        for j in others():
            fetch(j)
            pltpu.make_async_remote_copy(
                src_ref=stage.at[which, j],
                dst_ref=got.at[which, :, rows, columns],
                send_sem=send2.at[which],
                recv_sem=recv2.at[which],
                device_id=(j,),
                device_id_type=MESH,
            ).start()

    def part(which, turn, weights, at):
        return jnp.dot(weights, got[which, turn, :, at], preferred_element_type=F32)

    def merged(m0, t0, m1, t1):
        peak = jnp.maximum(m0, m1)
        f0, f1 = jnp.exp(m0 - peak), jnp.exp(m1 - peak)
        den = f0 * t0 + f1 * t1
        return f0, f1, 1.0 / den, to_row(peak + jnp.log(den))

    chunks = [slice(at, at + WIDE) for at in range(0, s_ref.shape[1], WIDE)]

    def side(which, query_ref, aligned_ref, row):
        pltpu.make_async_copy(got.at[which], got.at[which], recv2.at[which]).wait()
        queries = query_ref[...]
        m0, t0, p0 = weigh(queries, got[which, 0], factor)
        m1, t1, p1 = weigh(queries, got[which, 1], factor)
        f0, f1, inverse, lse = merged(m0, t0, m1, t1)
        for at in chunks:
            total = f0 * part(which, 0, p0, at) + f1 * part(which, 1, p1, at)
            aligned_ref[:, at] = (total * inverse).astype(BF)
        lse_ref[row : row + 1] = lse

    side(0, t_ref, to_ref, 1)
    side(1, s_ref, so_ref, 0)

    def sent(ref, sem):
        pltpu.make_async_remote_copy(
            src_ref=ref, dst_ref=ref, send_sem=sem, recv_sem=sem,
            device_id=(lax.rem(me + 1, DEVICES),), device_id_type=MESH,
        ).wait_send()

    for which, ref, held in sides:
        sent(held.at[pl.ds(0, DEVICES - 1)], send1.at[which])
        sent(stage.at[which, pl.ds(0, DEVICES - 1)], send2.at[which])


def hand_on(s_ref, t_ref, lse_ref, so_ref, to_ref, sl_ref, tl_ref):
    so_ref[...] = s_ref[...]
    to_ref[...] = t_ref[...]
    sl_ref[...] = lse_ref[0]
    tl_ref[...] = lse_ref[1]


def local(source, target, partner):
    rows, width = source.shape
    vmem = pl.BlockSpec(memory_space=pltpu.VMEM)
    anywhere = pl.BlockSpec(memory_space=pl.ANY)
    slab = jax.ShapeDtypeStruct((rows, width), BF)
    row = jax.ShapeDtypeStruct((rows,), F32)
    aligned_s, aligned_t, lse = pl.pallas_call(
        functools.partial(kernel, width ** (-0.5)),
        out_shape=(slab, slab, jax.ShapeDtypeStruct((2, rows), F32)),
        in_specs=[anywhere, anywhere, anywhere],
        out_specs=(vmem, vmem, vmem),
        scratch_shapes=[
            pltpu.SMEM(partner.shape, jnp.int32),
            pltpu.VMEM((rows, width), BF),
            pltpu.VMEM((rows, width), BF),
            pltpu.VMEM((DEVICES, 8, 128), BF),
            pltpu.VMEM((DEVICES, 8, 128), BF),
            pltpu.VMEM((2, DEVICES, 2, 8, 128), BF),
            pltpu.VMEM((2, 2, rows, width), BF),
            pltpu.SemaphoreType.DMA((2,)),
            pltpu.SemaphoreType.DMA((2,)),
            pltpu.SemaphoreType.DMA((2,)),
            pltpu.SemaphoreType.DMA((2,)),
            pltpu.SemaphoreType.DMA((3,)),
        ],
        compiler_params=pltpu.CompilerParams(
            collective_id=0, has_side_effects=True, vmem_limit_bytes=GRANT
        ),
    )(partner, source, target)
    return pl.pallas_call(
        hand_on,
        out_shape=(slab, slab, row, row),
        in_specs=[vmem, vmem, vmem],
        out_specs=(vmem, vmem, vmem, vmem),
        compiler_params=pltpu.CompilerParams(vmem_limit_bytes=GRANT),
    )(aligned_s, aligned_t, lse)


def solution(mesh):
    return jax.shard_map(
        local,
        mesh=mesh,
        in_specs=(P("dev", None), P("dev", None), P()),
        out_specs=(P("dev", None), P("dev", None), P("dev"), P("dev")),
        check_vma=False,
    )
```

```python
import functools

import jax
import jax.numpy as jnp
from jax import lax
from jax.experimental import pallas as pl
from jax.experimental.pallas import tpu as pltpu
from jax.sharding import PartitionSpec as P

MESH = pl.DeviceIdType.MESH
BF, F32 = jnp.bfloat16, jnp.float32
SIDE = 4
DEVICES = 2 * SIDE**3
WIDE = 256
GRANT = 54700 << 10
HOPS = (0, 1, 2, 1)
FAR_FIRST = sorted(
    ((z, y, x) for z in range(SIDE) for y in range(SIDE) for x in range(SIDE)),
    key=lambda offset: -sum(HOPS[step] for step in offset),
)[:-1]


def tile(device):
    row = pl.multiple_of(lax.div(device, 8) * 8, 8)
    column = pl.multiple_of(lax.rem(device, 8) * 128, 128)
    return pl.ds(row, 8), pl.ds(column, 128)


def away(place, offset):
    z, y, x = (lax.rem(at + step, SIDE) if step else at for at, step in zip(place, offset))
    return (SIDE * z + y) * SIDE + x


def weigh(queries, values, factor):
    scores = lax.dot_general(
        queries, values, (((1,), (1,)), ((), ())), preferred_element_type=F32
    ) * factor
    highest = jnp.max(scores, axis=1, keepdims=True)
    weights = jnp.exp(scores - highest)
    total = jnp.sum(weights, axis=1, keepdims=True)
    return highest, total, weights.astype(BF)


def to_row(column):
    rows = column.shape[0]
    at_row = lax.broadcasted_iota(jnp.int32, (rows, rows), 0)
    at_column = lax.broadcasted_iota(jnp.int32, (rows, rows), 1)
    spread = jnp.where(at_row == at_column, jnp.broadcast_to(column, (rows, rows)), 0.0)
    return jnp.sum(spread, axis=0, keepdims=True)


def kernel(
    factor, partner_hbm, s_hbm, t_hbm, so_ref, to_ref, lse_ref,
    partner, s_ref, t_ref, held_s, held_t, stage, got,
    send1, recv1, send2, recv2, in_sem,
):
    me = lax.axis_index("dev")
    chip, core = lax.div(me, 2), lax.rem(me, 2)
    place = tuple(lax.rem(lax.div(chip, unit), SIDE) for unit in (SIDE * SIDE, SIDE, 1))
    mate = 2 * chip + 1 - core
    rows, columns = tile(me)

    get_s = pltpu.make_async_copy(s_hbm, s_ref, in_sem.at[0])
    get_t = pltpu.make_async_copy(t_hbm, t_ref, in_sem.at[1])
    get_partner = pltpu.make_async_copy(partner_hbm, partner, in_sem.at[2])
    get_s.start()
    get_t.start()
    get_partner.start()

    barrier = pltpu.get_barrier_semaphore()

    def others():
        for offset in FAR_FIRST:
            first_core = 2 * away(place, offset)
            yield first_core
            yield first_core + 1
        yield mate

    for j in others():
        pl.semaphore_signal(barrier, inc=1, device_id=(j,), device_id_type=MESH)

    get_s.wait()
    get_t.wait()
    pl.semaphore_wait(barrier, DEVICES - 1)

    sides = ((0, s_ref, held_s), (1, t_ref, held_t))

    for which, ref, held in sides:
        pltpu.make_async_copy(
            ref.at[rows, columns], held.at[me], recv1.at[which]
        ).start()
        for j in others():
            at_rows, at_columns = tile(j)
            pltpu.make_async_remote_copy(
                src_ref=ref.at[at_rows, at_columns],
                dst_ref=held.at[me],
                send_sem=send1.at[which],
                recv_sem=recv1.at[which],
                device_id=(j,),
                device_id_type=MESH,
            ).start()

    get_partner.wait()
    for which, ref, held in sides:
        pltpu.make_async_copy(held, held, recv1.at[which]).wait()

        def fetch(j):
            for turn in range(2):
                stage[which, j, turn] = held[partner[turn, j]]

        fetch(me)
        pltpu.make_async_copy(
            stage.at[which, me], got.at[which, :, rows, columns], recv2.at[which]
        ).start()
        for j in others():
            fetch(j)
            pltpu.make_async_remote_copy(
                src_ref=stage.at[which, j],
                dst_ref=got.at[which, :, rows, columns],
                send_sem=send2.at[which],
                recv_sem=recv2.at[which],
                device_id=(j,),
                device_id_type=MESH,
            ).start()

    def part(which, turn, weights, at):
        return jnp.dot(weights, got[which, turn, :, at], preferred_element_type=F32)

    def merged(m0, t0, m1, t1):
        peak = jnp.maximum(m0, m1)
        f0, f1 = jnp.exp(m0 - peak), jnp.exp(m1 - peak)
        den = f0 * t0 + f1 * t1
        return f0, f1, 1.0 / den, to_row(peak + jnp.log(den))

    chunks = [slice(at, at + WIDE) for at in range(0, s_ref.shape[1], WIDE)]

    def side(which, query_ref, aligned_ref, row):
        pltpu.make_async_copy(got.at[which], got.at[which], recv2.at[which]).wait()
        queries = query_ref[...]
        m0, t0, p0 = weigh(queries, got[which, 0], factor)
        m1, t1, p1 = weigh(queries, got[which, 1], factor)
        f0, f1, inverse, lse = merged(m0, t0, m1, t1)
        for at in chunks:
            total = f0 * part(which, 0, p0, at) + f1 * part(which, 1, p1, at)
            aligned_ref[:, at] = (total * inverse).astype(BF)
        lse_ref[row : row + 1] = lse

    side(0, t_ref, to_ref, 1)
    side(1, s_ref, so_ref, 0)

    def sent(ref, sem):
        pltpu.make_async_remote_copy(
            src_ref=ref, dst_ref=ref, send_sem=sem, recv_sem=sem,
            device_id=(lax.rem(me + 1, DEVICES),), device_id_type=MESH,
        ).wait_send()

    for which, ref, held in sides:
        sent(held.at[pl.ds(0, DEVICES - 1)], send1.at[which])
        sent(stage.at[which, pl.ds(0, DEVICES - 1)], send2.at[which])


def hand_on(s_ref, t_ref, lse_ref, so_ref, to_ref, sl_ref, tl_ref):
    so_ref[...] = s_ref[...]
    to_ref[...] = t_ref[...]
    sl_ref[...] = lse_ref[0]
    tl_ref[...] = lse_ref[1]


def local(source, target, partner):
    rows, width = source.shape
    vmem = pl.BlockSpec(memory_space=pltpu.VMEM)
    anywhere = pl.BlockSpec(memory_space=pl.ANY)
    slab = jax.ShapeDtypeStruct((rows, width), BF)
    row = jax.ShapeDtypeStruct((rows,), F32)
    aligned_s, aligned_t, lse = pl.pallas_call(
        functools.partial(kernel, width ** (-0.5)),
        out_shape=(slab, slab, jax.ShapeDtypeStruct((2, rows), F32)),
        in_specs=[anywhere, anywhere, anywhere],
        out_specs=(vmem, vmem, vmem),
        scratch_shapes=[
            pltpu.SMEM(partner.shape, jnp.int32),
            pltpu.VMEM((rows, width), BF),
            pltpu.VMEM((rows, width), BF),
            pltpu.VMEM((DEVICES, 8, 128), BF),
            pltpu.VMEM((DEVICES, 8, 128), BF),
            pltpu.VMEM((2, DEVICES, 2, 8, 128), BF),
            pltpu.VMEM((2, 2, rows, width), BF),
            pltpu.SemaphoreType.DMA((2,)),
            pltpu.SemaphoreType.DMA((2,)),
            pltpu.SemaphoreType.DMA((2,)),
            pltpu.SemaphoreType.DMA((2,)),
            pltpu.SemaphoreType.DMA((3,)),
        ],
        compiler_params=pltpu.CompilerParams(
            collective_id=0, has_side_effects=True, vmem_limit_bytes=GRANT
        ),
    )(partner, source, target)
    return pl.pallas_call(
        hand_on,
        out_shape=(slab, slab, row, row),
        in_specs=[vmem, vmem, vmem],
        out_specs=(vmem, vmem, vmem, vmem),
        compiler_params=pltpu.CompilerParams(vmem_limit_bytes=GRANT),
    )(aligned_s, aligned_t, lse)


def solution(mesh):
    return jax.shard_map(
        local,
        mesh=mesh,
        in_specs=(P("dev", None), P("dev", None), P()),
        out_specs=(P("dev", None), P("dev", None), P("dev"), P("dev")),
        check_vma=False,
    )
```
